32 devices in a mesh: rep: 16 (over z, y, x), shard: 2 (over core).
Axes of the slice: x: 2, y: 2, z: 4, core: 2. Of those that a mesh axis runs over, the one named last changes fastest.
Arguments:
- grad_parts: float32 [16, 2, 2, 1024, 512], P('rep', 'shard'), may hold values from -6 to 6
- weights: bfloat16 [2, 1024, 512], P(None, 'shard'), may hold values from -3 to 3
- stat_left: float32 [2, 1024, 1024], P(None, 'shard'), may hold values from -12 to 332, as said below
- stat_right: float32 [512, 512], replicated, may hold values from -12 to 238.27417, as said below
- basis_left: bfloat16 [2, 1024, 1024], P(None, 'shard'), may hold values from -0.1875 to 0.1875
- basis_right: bfloat16 [512, 512], replicated, may hold values from -0.25 to 0.25
- moment_first: float32 [2, 1024, 512], P(None, 'shard'), may hold values from -2 to 2
- moment_second: float32 [2, 1024, 512], P(None, 'shard'), may hold values from 0.05 to 1
Outputs:
- weights_new: bfloat16 [2, 1024, 512], replicated
- basis_left_new: bfloat16 [2, 1024, 1024], P(None, 'shard')
- basis_right_new: bfloat16 [512, 512], replicated
- moment_first_new: float32 [2, 1024, 512], P(None, 'shard')
- moment_second_new: float32 [2, 1024, 512], P(None, 'shard')
The draws below stay inside these ranges and needn't reach their ends.
Inputs may be any that keep to these rules, and one draw needn't show every extreme that they name: `stat_left`: each block is a symmetric matrix. `stat_right`: a symmetric matrix.
All inputs are finite; a program needn't handle non-finite values.
Results may differ from the reference program's by a relative error of at most 0.015.
Values may be sent and summed in bfloat16 or wider, within the bound.
A program may use at most 128 MiB of HBM per device.

```python
import math
import jax
import jax.numpy as jnp
from jax import lax

D = 2048
KV = 512
BLK = 1024
NS_ITERS = 3
NBLK = 2
N_REP = 16
N_SHARD = 2


def symmetric_stat(key, block_count, block_size):
    key_noise = jax.random.fold_in(key, 11)
    key_diagonal = jax.random.fold_in(key, 12)
    noise_values = jnp.clip(jax.random.normal(key_noise, (block_count, block_size, block_size), jnp.float32), -3.0, 3.0)
    symmetric = 0.5 * (noise_values + jnp.swapaxes(noise_values, 1, 2))
    diagonal = jnp.exp(jax.random.uniform(key_diagonal, (block_count, block_size), jnp.float32, 0.0, math.log(10.0))) * math.sqrt(block_size)
    identity = (jnp.arange(block_size)[:, None] == jnp.arange(block_size)[None, :]).astype(jnp.float32)
    return symmetric + identity[None, :, :] * diagonal[:, :, None]


def draw_stat_left(key, part):
    return symmetric_stat(key, D // BLK, BLK)


def draw_stat_right(key, part):
    return symmetric_stat(key, 1, KV).reshape(KV, KV)


def spiked(result, rng, source, target, parts, factor):
    def block_of(position):
        return (jnp.arange(result.shape[position]) // (result.shape[position] // parts)).reshape((-1,) + (1,) * (result.ndim - 1 - position))

    first = jax.random.permutation(rng, parts)[block_of(target)]
    far = (block_of(target) + parts // 2) % parts
    return jnp.where((block_of(source) == first) | (block_of(source) == far), factor * result, result)


def shard_levels(rng, shape, shards, low, high):
    factor_of = 1.0
    for axis_at, blocks in shards:
        steps = jax.random.uniform(jax.random.fold_in(jax.random.fold_in(rng, 6), axis_at), (blocks,), jnp.float32, low / len(shards), high / len(shards))
        factor_of = factor_of * jnp.repeat(jnp.exp(steps), shape[axis_at] // blocks).reshape((-1,) + (1,) * (len(shape) - 1 - axis_at))
    return factor_of


def gaussian(own_key, dims, scale, bound, pieces=(), dtype=jnp.bfloat16):
    gain = shard_levels(own_key, dims, pieces, -0.22, 0.18) if pieces else 1.0
    result = jax.random.normal(own_key, dims, jnp.float32) * scale * gain
    return jnp.minimum(jnp.maximum(result, -bound), bound).astype(dtype)


def bell_draw_with(key, extent, width, bound, pieces, heavy, dtype=jnp.bfloat16):
    drawn = width * jax.random.normal(key, extent, jnp.float32)
    if pieces:
        drawn = drawn * shard_levels(key, extent, pieces, -0.22, 0.18)
    return jnp.clip(spiked(drawn, jax.random.fold_in(key, 3), *heavy), -bound, bound).astype(dtype)


def setup_inputs(seed: int = 0) -> dict:
    keys = jax.random.split(jax.random.key(seed), 9)
    return {
        "grad_parts": bell_draw_with(keys[0], (N_REP, N_SHARD, NBLK, BLK, KV), 1.0, 6.0, ((0, 16), (1, 2)), (1, 3, 2, 2.0), jnp.float32),
        "weights": gaussian(keys[1], (NBLK, BLK, KV), 0.5, 3.0, ((1, 2),)),
        "stat_left": draw_stat_left(jax.random.fold_in(keys[8], 71), 0),
        "stat_right": draw_stat_right(jax.random.fold_in(keys[8], 71), 0),
        "basis_left": gaussian(keys[4], (NBLK, BLK, BLK), BLK ** -0.5, 0.1875, ((1, 2),)),
        "basis_right": gaussian(keys[5], (KV, KV), KV ** -0.5, 0.25),
        "moment_first": gaussian(keys[6], (NBLK, BLK, KV), 0.3, 2.0, ((1, 2),), jnp.float32),
        "moment_second": jnp.clip(jnp.exp(math.log(1.0) - 2.9957323 * jax.random.uniform(keys[7], (NBLK, BLK, KV), jnp.float32) ** shard_levels(keys[7], (NBLK, BLK, KV), ((1, 2),), -0.2, 0.2)), 0.05, 1.0),
    }


stat_beta = 0.9
moment_decay = 0.9
square_decay = 0.95
learn_rate = 0.1
epsilon = 1e-08
norm_epsilon = 1e-06
schulz_linear = 3.4445
schulz_cubic = -4.775
schulz_quintic = 2.0315

def schulz(matrix):
    current = matrix
    for sweep_index in range(NS_ITERS):
        gram_matrix = lax.optimization_barrier(jnp.dot(current, current.T, preferred_element_type=jnp.float32).astype(jnp.bfloat16))
        poly_matrix = (schulz_cubic * gram_matrix.astype(jnp.float32) + schulz_quintic * jnp.dot(gram_matrix, gram_matrix, preferred_element_type=jnp.float32)).astype(jnp.bfloat16)
        current = (schulz_linear * current.astype(jnp.float32) + jnp.dot(poly_matrix, current, preferred_element_type=jnp.float32)).astype(jnp.bfloat16)
    return current

def power_start(statistic, basis_old):
    power_rows = jnp.dot(statistic.astype(jnp.bfloat16), basis_old, preferred_element_type=jnp.float32)
    return (power_rows * lax.rsqrt(jnp.sum(power_rows * power_rows) + norm_epsilon)).astype(jnp.bfloat16)

def reference(grad_parts, weights, stat_left, stat_right, basis_left, basis_right, moment_first, moment_second):
    grad_mean = lax.optimization_barrier(jnp.sum(grad_parts, axis=(0, 1))) / N_REP
    grad_low = grad_mean.astype(jnp.bfloat16)
    grad_flat = grad_low.reshape(D, KV)
    right_new = stat_beta * stat_right + (1.0 - stat_beta) * jnp.dot(grad_flat.T, grad_flat, preferred_element_type=jnp.float32)
    basis_right_new = schulz(power_start(right_new, basis_right))
    left_blocks = []
    rotate_blocks = []
    for block_index in range(D // BLK):
        grad_block = grad_low[block_index]
        left_new = stat_beta * stat_left[block_index] + (1.0 - stat_beta) * jnp.dot(grad_block, grad_block.T, preferred_element_type=jnp.float32)
        left_blocks.append(schulz(power_start(left_new, basis_left[block_index])))
        rotate_blocks.append(jnp.dot(basis_left[block_index].T, grad_block, preferred_element_type=jnp.float32))
    rot_left = jnp.stack(rotate_blocks, 0)
    rotated = jnp.dot(rot_left.reshape(D, KV).astype(jnp.bfloat16), basis_right, preferred_element_type=jnp.float32).reshape(D // BLK, BLK, KV)
    moment_new = moment_decay * moment_first + (1.0 - moment_decay) * rotated
    square_new = square_decay * moment_second + (1.0 - square_decay) * rotated * rotated
    direction = moment_new / (jnp.sqrt(square_new) + epsilon)
    half_turn = jnp.dot(direction.reshape(D, KV).astype(jnp.bfloat16), basis_right.T, preferred_element_type=jnp.float32).astype(jnp.bfloat16).reshape(D // BLK, BLK, KV)
    update_blocks = []
    for block_index in range(D // BLK):
        update_blocks.append(jnp.dot(basis_left[block_index], half_turn[block_index], preferred_element_type=jnp.float32))
    update = jnp.stack(update_blocks, 0)
    weights_new = (weights.astype(jnp.float32) - learn_rate * update).astype(jnp.bfloat16)
    return (weights_new, jnp.stack(left_blocks, 0), basis_right_new, moment_new, square_new)
```

```python
import functools

import jax
import jax.numpy as jnp
from jax import lax
from jax.experimental import pallas as pl
from jax.experimental.pallas import tpu as pltpu
from jax.sharding import PartitionSpec as P

NS_ITERS = 3


stat_beta = 0.9
moment_decay = 0.9
square_decay = 0.95
learn_rate = 0.1
epsilon = 1e-08
norm_epsilon = 1e-06
schulz_linear = 3.4445
schulz_cubic = -4.775
schulz_quintic = 2.0315


def schulz_whole(matrix):
    current = matrix
    for sweep_index in range(NS_ITERS):
        gram_matrix = lax.optimization_barrier(
            jnp.dot(current, current.T, preferred_element_type=jnp.float32).astype(jnp.bfloat16)
        )
        poly_matrix = (
            schulz_cubic * gram_matrix.astype(jnp.float32)
            + schulz_quintic * jnp.dot(gram_matrix, gram_matrix, preferred_element_type=jnp.float32)
        ).astype(jnp.bfloat16)
        current = (
            schulz_linear * current.astype(jnp.float32)
            + jnp.dot(poly_matrix, current, preferred_element_type=jnp.float32)
        ).astype(jnp.bfloat16)
    return current


def schulz_split(start_rows):
    current = start_rows
    for sweep_index in range(NS_ITERS):
        gathered = lax.all_gather(current, "shard", axis=1, tiled=True)
        gram_rows = lax.optimization_barrier(
            jnp.einsum(
                "bik,bjk->bij", current, gathered, preferred_element_type=jnp.float32
            ).astype(jnp.bfloat16)
        )
        gram_block = lax.all_gather(gram_rows, "shard", axis=1, tiled=True)
        poly_rows = (
            schulz_cubic * gram_rows.astype(jnp.float32)
            + schulz_quintic
            * jnp.einsum("bij,bjk->bik", gram_rows, gram_block, preferred_element_type=jnp.float32)
        ).astype(jnp.bfloat16)
        current = (
            schulz_linear * current.astype(jnp.float32)
            + jnp.einsum("bij,bjk->bik", poly_rows, gathered, preferred_element_type=jnp.float32)
        ).astype(jnp.bfloat16)
    return current


def on_device(
    grad_parts, weights, stat_left, stat_right, basis_left, basis_right, moment_first, moment_second
):
    block_count = weights.shape[0]
    row_count = weights.shape[1]
    width_kv = weights.shape[2]
    rep_count = lax.axis_size("rep")
    shard_pos = lax.axis_index("shard")
    row_start = shard_pos * row_count
    partial_value = grad_parts[0, 0]
    grad_total = lax.psum(partial_value, ("rep", "shard")) / rep_count
    grad_full = grad_total.astype(jnp.bfloat16)
    grad_rows = lax.dynamic_slice_in_dim(grad_full, row_start, row_count, 1)
    left_new = stat_beta * stat_left + (1.0 - stat_beta) * jnp.einsum(
        "bik,bjk->bij", grad_rows, grad_full, preferred_element_type=jnp.float32
    )
    grad_flat = grad_rows.reshape(block_count * row_count, width_kv)
    right_terms = jnp.dot(grad_flat.T, grad_flat, preferred_element_type=jnp.float32)
    right_new = stat_beta * stat_right + (1.0 - stat_beta) * lax.psum(right_terms, "shard")
    basis_all = lax.all_gather(basis_left, "shard", axis=1, tiled=True)
    power_rows = jnp.einsum(
        "bij,bjk->bik", left_new.astype(jnp.bfloat16), basis_all, preferred_element_type=jnp.float32
    )
    local_squares = jnp.sum(power_rows * power_rows, axis=(1, 2))
    block_squares = lax.psum(local_squares, "shard")
    start_rows = (power_rows * lax.rsqrt(block_squares + norm_epsilon)[:, None, None]).astype(
        jnp.bfloat16
    )
    basis_left_new = schulz_split(start_rows)
    right_power = jnp.dot(
        right_new.astype(jnp.bfloat16), basis_right, preferred_element_type=jnp.float32
    )
    right_start = (
        right_power * lax.rsqrt(jnp.sum(right_power * right_power) + norm_epsilon)
    ).astype(jnp.bfloat16)
    basis_right_new = schulz_whole(right_start)
    local_turn = jnp.einsum(
        "bji,bjk->bik", basis_left, grad_rows, preferred_element_type=jnp.float32
    )
    rot_left = lax.psum_scatter(
        local_turn.astype(jnp.bfloat16), "shard", scatter_dimension=1, tiled=True
    ).astype(jnp.float32)
    rot_flat = rot_left.reshape(block_count * row_count, width_kv).astype(jnp.bfloat16)
    rotated = jnp.dot(rot_flat, basis_right, preferred_element_type=jnp.float32).reshape(
        block_count, row_count, width_kv
    )
    moment_new = moment_decay * moment_first + (1.0 - moment_decay) * rotated
    square_new = square_decay * moment_second + (1.0 - square_decay) * rotated * rotated
    direction = moment_new / (jnp.sqrt(square_new) + epsilon)
    direction_flat = direction.reshape(block_count * row_count, width_kv).astype(jnp.bfloat16)
    half_turn = (
        jnp.dot(direction_flat, basis_right.T, preferred_element_type=jnp.float32)
        .astype(jnp.bfloat16)
        .reshape(block_count, row_count, width_kv)
    )
    half_all = lax.all_gather(half_turn, "shard", axis=1, tiled=True)
    update = jnp.einsum("bij,bjk->bik", basis_left, half_all, preferred_element_type=jnp.float32)
    weight_rows_new = (weights.astype(jnp.float32) - learn_rate * update).astype(jnp.bfloat16)
    weights_new = lax.all_gather(weight_rows_new, "shard", axis=1, tiled=True)
    return (weights_new, basis_left_new, basis_right_new, moment_new, square_new)


MESH = pl.DeviceIdType.MESH
PLANE = 4
LINE = 4
ORDER = (2, 1, 3, 0)
F32 = jnp.float32
BF16 = jnp.bfloat16


def gather_kernel(
    parts, basis, stat, first, second, weights,
    grad_out, basis_out, stat_out, first_out, second_out, weights_out,
    far_part, near_part, pair_send, pair_recv, chip_low, plane_recv, line_send, line_recv,
    load_sem, pair_sem, plane_sem, line_sem, gline_sem, gplane_sem, gpair_sem, swap_sem, keep_sem,
):
    rep = lax.axis_index("rep")
    core = lax.axis_index("shard")
    other = 1 - core
    layer = rep // PLANE
    spot = lax.rem(rep, PLANE)
    height = basis.shape[1]

    def line_of(k):
        return lax.rem(layer + k, LINE)

    def spot_of(j):
        return lax.rem(spot + j, PLANE)

    loads = {}
    for k in ORDER:
        far = pltpu.make_async_copy(parts.at[other, :, line_of(k)], far_part.at[k], load_sem.at[0, k])
        near = pltpu.make_async_copy(parts.at[core, :, line_of(k)], near_part.at[k], load_sem.at[1, k])
        far.start()
        near.start()
        loads[k] = (far, near)

    barrier = pltpu.get_barrier_semaphore()
    partners = [(rep, other)]
    partners += [(layer * PLANE + spot_of(j), core) for j in range(1, PLANE)]
    partners += [(line_of(k) * PLANE + spot, core) for k in range(1, LINE)]
    for partner in partners:
        pl.semaphore_signal(barrier, inc=1, device_id=partner, device_id_type=MESH)
    pl.semaphore_wait(barrier, len(partners))

    def send(source, target, sems, partner):
        copy = pltpu.make_async_remote_copy(
            src_ref=source, dst_ref=target, send_sem=sems.at[0], recv_sem=sems.at[1],
            device_id=partner, device_id_type=MESH,
        )
        copy.start()
        return copy

    sent = []
    pairs = {}
    for k in ORDER:
        loads[k][0].wait()
        pair_send[k] = far_part[k].astype(BF16)
        pairs[k] = send(pair_send.at[k], pair_recv.at[k], pair_sem.at[k], (rep, other))

    planes = {}
    for k in ORDER:
        loads[k][1].wait()
        pairs[k].wait_recv()
        near_part[k] = near_part[k] + pair_recv[k].astype(F32)
        chip_low[k] = near_part[k].astype(BF16)
        for j in (2, 1, 3):
            planes[k, j] = send(
                chip_low.at[k, spot_of(j)], plane_recv.at[k, j - 1], plane_sem.at[k, j - 1],
                (layer * PLANE + spot_of(j), core),
            )

    mine = pl.ds(pl.multiple_of(core * height, height), height)
    swaps = []
    keeps = []
    moved = ((basis, basis_out), (stat, stat_out), (first, first_out), (second, second_out), (weights, weights_out))
    for at, (source, target) in enumerate(moved):
        swaps.append(send(source.at[other], target.at[mine], swap_sem.at[at], (rep, other)))
        keep = pltpu.make_async_copy(source.at[core], target.at[mine], keep_sem.at[at])
        keep.start()
        keeps.append(keep)

    lines = {}
    total = None
    for k in ORDER:
        for j in range(1, PLANE):
            planes[k, j].wait_recv()
        total = near_part[k, spot]
        for j in range(1, PLANE):
            total = total + plane_recv[k, j - 1].astype(F32)
        if k:
            line_send[k - 1] = total.astype(BF16)
            lines[k] = send(
                line_send.at[k - 1], line_recv.at[k - 1], line_sem.at[k - 1],
                (line_of(k) * PLANE + spot, core),
            )
    for k in range(1, LINE):
        lines[k].wait_recv()
        total = total + line_recv[k - 1].astype(F32)
    grad_out[core, spot, layer] = (total * (1.0 / (PLANE * LINE))).astype(BF16)

    def share(piece, sems, partner):
        return send(grad_out.at[piece], grad_out.at[piece], sems, partner)

    own = (core, spot, layer)
    glines = {k: share(own, gline_sem.at[k - 1], (line_of(k) * PLANE + spot, core)) for k in (2, 1, 3)}
    gplanes = {}
    gpairs = []
    for k in (0, 1, 3, 2):
        piece = (core, spot, lax.rem(layer + LINE - k, LINE))
        if k:
            glines[k].wait_recv()
        for j in (2, 1, 3):
            gplanes[k, j] = share(piece, gplane_sem.at[k, j - 1], (layer * PLANE + spot_of(j), core))
        gpairs.append(share(piece, gpair_sem.at[k, 0], (rep, other)))
    for k in (0, 1, 3, 2):
        for j in (1, 3, 2):
            gplanes[k, j].wait_recv()
            piece = (core, lax.rem(spot + PLANE - j, PLANE), lax.rem(layer + LINE - k, LINE))
            gpairs.append(share(piece, gpair_sem.at[k, j], (rep, other)))
    for copy in gpairs + swaps:
        copy.wait_recv()
    for group in (pairs, planes, lines, glines, gplanes):
        sent += list(group.values())
    for copy in sent + gpairs + swaps:
        copy.wait_send()
    for keep in keeps:
        keep.wait()


def gather_inputs(grad_parts, basis, stat, first, second, weights):
    blocks, height, width = weights.shape
    block = 2 * height
    piece = block // (PLANE * LINE)
    parts = grad_parts.reshape(blocks, PLANE, LINE, piece, width)
    anywhere = pl.BlockSpec(memory_space=pl.ANY)
    dma = pltpu.SemaphoreType.DMA
    out = pl.pallas_call(
        gather_kernel,
        out_shape=(
            jax.ShapeDtypeStruct((blocks, PLANE, LINE, piece, width), BF16),
            jax.ShapeDtypeStruct((block, block), BF16),
            jax.ShapeDtypeStruct((block, block), F32),
            jax.ShapeDtypeStruct((block, width), F32),
            jax.ShapeDtypeStruct((block, width), F32),
            jax.ShapeDtypeStruct((block, width), BF16),
        ),
        in_specs=[anywhere] * 6,
        out_specs=(pl.BlockSpec(memory_space=pltpu.VMEM),) + (anywhere,) * 5,
        scratch_shapes=[
            pltpu.VMEM((LINE, PLANE, piece, width), F32),
            pltpu.VMEM((LINE, PLANE, piece, width), F32),
            pltpu.VMEM((LINE, PLANE, piece, width), BF16),
            pltpu.VMEM((LINE, PLANE, piece, width), BF16),
            pltpu.VMEM((LINE, PLANE, piece, width), BF16),
            pltpu.VMEM((LINE, PLANE - 1, piece, width), BF16),
            pltpu.VMEM((LINE - 1, piece, width), BF16),
            pltpu.VMEM((LINE - 1, piece, width), BF16),
            dma((2, LINE)),
            dma((LINE, 2)),
            dma((LINE, PLANE - 1, 2)),
            dma((LINE - 1, 2)),
            dma((LINE - 1, 2)),
            dma((LINE, PLANE - 1, 2)),
            dma((LINE, PLANE, 2)),
            dma((5, 2)),
            dma((5,)),
        ],
        compiler_params=pltpu.CompilerParams(
            collective_id=0, has_side_effects=True, vmem_limit_bytes=40 << 20
        ),
    )(parts, basis, stat, first, second, weights)
    return (out[0].reshape(blocks, block, width),) + tuple(out[1:])


def dot(a, b, dims=((1,), (0,))):
    return lax.dot_general(a, b, (dims, ((), ())), preferred_element_type=F32)


def turn_kernel(grad, basis, right, first, second, weights, first_out, second_out, weights_out, half):
    core = lax.axis_index("shard")
    tile = 256

    @pl.loop(0, basis.shape[0] // tile)
    def _(at):
        rows = pl.ds(pl.multiple_of(at * tile, tile), tile)
        rot = dot(basis[:, rows], grad[core], ((0,), (0,)))
        rotated = dot(rot.astype(BF16), right[...])
        moment = moment_decay * first[rows, :] + (1.0 - moment_decay) * rotated
        square = square_decay * second[rows, :] + (1.0 - square_decay) * rotated * rotated
        first_out[rows, :] = moment
        second_out[rows, :] = square
        direction = moment / (jnp.sqrt(square) + epsilon)
        half[rows, :] = dot(direction.astype(BF16), right[...], ((1,), (1,))).astype(BF16)

    @pl.loop(0, basis.shape[0] // tile)
    def _(at):
        rows = pl.ds(pl.multiple_of(at * tile, tile), tile)
        update = dot(basis[rows, :], half[...])
        weights_out[rows, :] = (weights[rows, :].astype(F32) - learn_rate * update).astype(BF16)


def turn_block(grad, basis, right, first, second, weights):
    in_vmem = pl.BlockSpec(memory_space=pltpu.VMEM)
    return pl.pallas_call(
        turn_kernel,
        out_shape=(
            jax.ShapeDtypeStruct(first.shape, F32),
            jax.ShapeDtypeStruct(second.shape, F32),
            jax.ShapeDtypeStruct(weights.shape, BF16),
        ),
        in_specs=[in_vmem] * 6,
        out_specs=(in_vmem,) * 3,
        scratch_shapes=[pltpu.VMEM(weights.shape, BF16)],
        compiler_params=pltpu.CompilerParams(vmem_limit_bytes=40 << 20),
        cost_estimate=pl.CostEstimate(flops=3 << 30, bytes_accessed=16 << 20, transcendentals=0),
    )(grad, basis, right, first, second, weights)


def schulz_sweeps(start, gram, spare, out, size, tile):
    tiles = size // tile
    chain = [start, spare, start, out]
    for sweep in range(NS_ITERS):
        now, later = chain[sweep], (out if sweep == NS_ITERS - 1 else chain[sweep + 1])

        @pl.loop(0, tiles)
        def _(at):
            rows = pl.ds(pl.multiple_of(at * tile, tile), tile)
            gram[rows, :] = dot(now[rows, :], now[...], ((1,), (1,))).astype(BF16)

        @pl.loop(0, tiles)
        def _(at):
            rows = pl.ds(pl.multiple_of(at * tile, tile), tile)
            poly = schulz_cubic * gram[rows, :].astype(F32) + schulz_quintic * dot(gram[rows, :], gram[...])
            later[rows, :] = (
                schulz_linear * now[rows, :].astype(F32) + dot(poly.astype(BF16), now[...])
            ).astype(BF16)


def basis_kernel(
    grad, stat, basis, stat_right, right, left_out, right_out,
    power, start, spare, gram, rpower, rstart, rspare, rgram,
):
    core = lax.axis_index("shard")
    size = basis.shape[0]
    width = right.shape[0]
    tile = 256

    def left_tile(at, total):
        rows = pl.ds(pl.multiple_of(at * tile, tile), tile)
        mixed = stat_beta * stat[rows, :] + (1.0 - stat_beta) * dot(
            grad[core, rows, :], grad[core], ((1,), (1,))
        )
        value = dot(mixed.astype(BF16), basis[...])
        power[rows, :] = value
        return total + jnp.sum(value * value)

    total = lax.fori_loop(0, size // tile, left_tile, jnp.float32(0.0))
    scale = lax.rsqrt(total + norm_epsilon)

    @pl.loop(0, size // tile)
    def _(at):
        rows = pl.ds(pl.multiple_of(at * tile, tile), tile)
        start[rows, :] = (power[rows, :] * scale).astype(BF16)

    schulz_sweeps(start, gram, spare, left_out, size, tile)

    def right_tile(at, total):
        rows = pl.ds(pl.multiple_of(at * tile, tile), tile)
        terms = dot(grad[0, :, rows], grad[0], ((0,), (0,))) + dot(grad[1, :, rows], grad[1], ((0,), (0,)))
        mixed = stat_beta * stat_right[rows, :] + (1.0 - stat_beta) * terms
        value = dot(mixed.astype(BF16), right[...])
        rpower[rows, :] = value
        return total + jnp.sum(value * value)

    rtotal = lax.fori_loop(0, width // tile, right_tile, jnp.float32(0.0))
    rscale = lax.rsqrt(rtotal + norm_epsilon)
    rstart[...] = (rpower[...] * rscale).astype(BF16)
    schulz_sweeps(rstart, rgram, rspare, right_out, width, tile)


def new_bases(grad, stat, basis, stat_right, right):
    in_vmem = pl.BlockSpec(memory_space=pltpu.VMEM)
    size, width = basis.shape[0], right.shape[0]
    return pl.pallas_call(
        basis_kernel,
        out_shape=(jax.ShapeDtypeStruct(basis.shape, BF16), jax.ShapeDtypeStruct(right.shape, BF16)),
        in_specs=[in_vmem] * 5,
        out_specs=(in_vmem,) * 2,
        scratch_shapes=[
            pltpu.VMEM((size, size), F32),
            pltpu.VMEM((size, size), BF16),
            pltpu.VMEM((size, size), BF16),
            pltpu.VMEM((size, size), BF16),
            pltpu.VMEM((width, width), F32),
            pltpu.VMEM((width, width), BF16),
            pltpu.VMEM((width, width), BF16),
            pltpu.VMEM((width, width), BF16),
        ],
        compiler_params=pltpu.CompilerParams(vmem_limit_bytes=48 << 20),
        cost_estimate=pl.CostEstimate(flops=26 << 30, bytes_accessed=16 << 20, transcendentals=0),
    )(grad, stat, basis, stat_right, right)


def on_device_blocks(
    grad_parts, weights, stat_left, stat_right, basis_left, basis_right, moment_first, moment_second
):
    height = weights.shape[1]
    core = lax.axis_index("shard")
    grad, basis, stat, first, second, rows = gather_inputs(
        grad_parts, basis_left, stat_left, moment_first, moment_second, weights
    )
    first_new, second_new, weights_block = turn_block(grad, basis, basis_right, first, second, rows)

    def halves(value):
        keep = lax.dynamic_slice_in_dim(value, core * height, height, 0)
        give = lax.dynamic_slice_in_dim(value, (1 - core) * height, height, 0)
        take = lax.ppermute(give, "shard", ((0, 1), (1, 0)))
        return join(keep, take)

    def join(keep, take):
        low = jnp.where(core == 0, keep, take)
        high = jnp.where(core == 0, take, keep)
        return jnp.stack((low, high))

    moment_new = halves(first_new)
    square_new = halves(second_new)
    weights_new = join(weights_block, lax.ppermute(weights_block, "shard", ((0, 1), (1, 0))))
    left_block, basis_right_new = new_bases(grad, stat, basis, stat_right, basis_right)
    basis_left_new = halves(left_block)
    return (weights_new, basis_left_new, basis_right_new, moment_new, square_new)


def solution(mesh):
    fits = mesh.shape["shard"] == 2 and mesh.shape["rep"] == 16
    body = on_device_blocks if fits else on_device
    placed = (
        P("rep", "shard", None, None, None),
        P(None, "shard", None),
        P(None, "shard", None),
        P(),
        P(None, "shard", None),
        P(),
        P(None, "shard", None),
        P(None, "shard", None),
    )
    return jax.shard_map(
        body,
        mesh=mesh,
        in_specs=placed,
        out_specs=(
            P(),
            P(None, "shard", None),
            P(),
            P(None, "shard", None),
            P(None, "shard", None),
        ),
        check_vma=False,
    )
```

```python
import functools

import jax
import jax.numpy as jnp
from jax import lax
from jax.experimental import pallas as pl
from jax.experimental.pallas import tpu as pltpu
from jax.sharding import PartitionSpec as P

NS_ITERS = 3


stat_beta = 0.9
moment_decay = 0.9
square_decay = 0.95
learn_rate = 0.1
epsilon = 1e-08
norm_epsilon = 1e-06
schulz_linear = 3.4445
schulz_cubic = -4.775
schulz_quintic = 2.0315


def schulz_whole(matrix):
    current = matrix
    for sweep_index in range(NS_ITERS):
        gram_matrix = lax.optimization_barrier(
            jnp.dot(current, current.T, preferred_element_type=jnp.float32).astype(jnp.bfloat16)
        )
        poly_matrix = (
            schulz_cubic * gram_matrix.astype(jnp.float32)
            + schulz_quintic * jnp.dot(gram_matrix, gram_matrix, preferred_element_type=jnp.float32)
        ).astype(jnp.bfloat16)
        current = (
            schulz_linear * current.astype(jnp.float32)
            + jnp.dot(poly_matrix, current, preferred_element_type=jnp.float32)
        ).astype(jnp.bfloat16)
    return current


def schulz_split(start_rows):
    current = start_rows
    for sweep_index in range(NS_ITERS):
        gathered = lax.all_gather(current, "shard", axis=1, tiled=True)
        gram_rows = lax.optimization_barrier(
            jnp.einsum(
                "bik,bjk->bij", current, gathered, preferred_element_type=jnp.float32
            ).astype(jnp.bfloat16)
        )
        gram_block = lax.all_gather(gram_rows, "shard", axis=1, tiled=True)
        poly_rows = (
            schulz_cubic * gram_rows.astype(jnp.float32)
            + schulz_quintic
            * jnp.einsum("bij,bjk->bik", gram_rows, gram_block, preferred_element_type=jnp.float32)
        ).astype(jnp.bfloat16)
        current = (
            schulz_linear * current.astype(jnp.float32)
            + jnp.einsum("bij,bjk->bik", poly_rows, gathered, preferred_element_type=jnp.float32)
        ).astype(jnp.bfloat16)
    return current


def on_device(
    grad_parts, weights, stat_left, stat_right, basis_left, basis_right, moment_first, moment_second
):
    block_count = weights.shape[0]
    row_count = weights.shape[1]
    width_kv = weights.shape[2]
    rep_count = lax.axis_size("rep")
    shard_pos = lax.axis_index("shard")
    row_start = shard_pos * row_count
    partial_value = grad_parts[0, 0]
    grad_total = lax.psum(partial_value, ("rep", "shard")) / rep_count
    grad_full = grad_total.astype(jnp.bfloat16)
    grad_rows = lax.dynamic_slice_in_dim(grad_full, row_start, row_count, 1)
    left_new = stat_beta * stat_left + (1.0 - stat_beta) * jnp.einsum(
        "bik,bjk->bij", grad_rows, grad_full, preferred_element_type=jnp.float32
    )
    grad_flat = grad_rows.reshape(block_count * row_count, width_kv)
    right_terms = jnp.dot(grad_flat.T, grad_flat, preferred_element_type=jnp.float32)
    right_new = stat_beta * stat_right + (1.0 - stat_beta) * lax.psum(right_terms, "shard")
    basis_all = lax.all_gather(basis_left, "shard", axis=1, tiled=True)
    power_rows = jnp.einsum(
        "bij,bjk->bik", left_new.astype(jnp.bfloat16), basis_all, preferred_element_type=jnp.float32
    )
    local_squares = jnp.sum(power_rows * power_rows, axis=(1, 2))
    block_squares = lax.psum(local_squares, "shard")
    start_rows = (power_rows * lax.rsqrt(block_squares + norm_epsilon)[:, None, None]).astype(
        jnp.bfloat16
    )
    basis_left_new = schulz_split(start_rows)
    right_power = jnp.dot(
        right_new.astype(jnp.bfloat16), basis_right, preferred_element_type=jnp.float32
    )
    right_start = (
        right_power * lax.rsqrt(jnp.sum(right_power * right_power) + norm_epsilon)
    ).astype(jnp.bfloat16)
    basis_right_new = schulz_whole(right_start)
    local_turn = jnp.einsum(
        "bji,bjk->bik", basis_left, grad_rows, preferred_element_type=jnp.float32
    )
    rot_left = lax.psum_scatter(
        local_turn.astype(jnp.bfloat16), "shard", scatter_dimension=1, tiled=True
    ).astype(jnp.float32)
    rot_flat = rot_left.reshape(block_count * row_count, width_kv).astype(jnp.bfloat16)
    rotated = jnp.dot(rot_flat, basis_right, preferred_element_type=jnp.float32).reshape(
        block_count, row_count, width_kv
    )
    moment_new = moment_decay * moment_first + (1.0 - moment_decay) * rotated
    square_new = square_decay * moment_second + (1.0 - square_decay) * rotated * rotated
    direction = moment_new / (jnp.sqrt(square_new) + epsilon)
    direction_flat = direction.reshape(block_count * row_count, width_kv).astype(jnp.bfloat16)
    half_turn = (
        jnp.dot(direction_flat, basis_right.T, preferred_element_type=jnp.float32)
        .astype(jnp.bfloat16)
        .reshape(block_count, row_count, width_kv)
    )
    half_all = lax.all_gather(half_turn, "shard", axis=1, tiled=True)
    update = jnp.einsum("bij,bjk->bik", basis_left, half_all, preferred_element_type=jnp.float32)
    weight_rows_new = (weights.astype(jnp.float32) - learn_rate * update).astype(jnp.bfloat16)
    weights_new = lax.all_gather(weight_rows_new, "shard", axis=1, tiled=True)
    return (weights_new, basis_left_new, basis_right_new, moment_new, square_new)


MESH = pl.DeviceIdType.MESH
PLANE = 4
LINE = 4
ORDER = (2, 1, 3, 0)
F32 = jnp.float32
BF16 = jnp.bfloat16


def dot(a, b, dims=((1,), (0,))):
    return lax.dot_general(a, b, (dims, ((), ())), preferred_element_type=F32)


def tile_rows(at, tile):
    return pl.ds(pl.multiple_of(at * tile, tile), tile)


def schulz_sweeps(start, gram, spare, size, tile):
    chain = (start, spare, start, spare)
    for sweep in range(NS_ITERS):
        now, later = chain[sweep % 2], chain[sweep % 2 + 1]

        @pl.loop(0, size // tile)
        def _(at):
            rows = tile_rows(at, tile)
            gram[rows, :] = dot(now[rows, :], now[...], ((1,), (1,))).astype(BF16)

        @pl.loop(0, size // tile)
        def _(at):
            rows = tile_rows(at, tile)
            poly = schulz_cubic * gram[rows, :].astype(F32) + schulz_quintic * dot(gram[rows, :], gram[...])
            later[rows, :] = (
                schulz_linear * now[rows, :].astype(F32) + dot(poly.astype(BF16), now[...])
            ).astype(BF16)
    return later


def step_kernel(
    parts, weights_in, stat_in, stat_right, basis_in, right, first_in, second_in,
    weights_out, basis_out, right_out, first_out, second_out,
    far_part, near_part, pair_send, pair_recv, chip_low, plane_recv, line_send, line_recv,
    grad, basis, stat, first, second, weights,
    power, rot, half, start, spare, gram, rpower, rstart, rspare, rgram,
    load_sem, pair_sem, plane_sem, line_sem, gline_sem, gplane_sem, gpair_sem, swap_sem, keep_sem,
    give_sem, store_sem,
):
    rep = lax.axis_index("rep")
    core = lax.axis_index("shard")
    other = 1 - core
    layer = rep // PLANE
    spot = lax.rem(rep, PLANE)
    size = basis.shape[0]
    height = basis_in.shape[1]
    piece = size // (PLANE * LINE)
    tile = 256

    def line_of(k):
        return lax.rem(layer + k, LINE)

    def spot_of(j):
        return lax.rem(spot + j, PLANE)

    def rows_of(p, z):
        return pl.ds(pl.multiple_of((p * LINE + z) * piece, piece), piece)

    loads = {}
    for k in ORDER:
        far = pltpu.make_async_copy(parts.at[other, :, line_of(k)], far_part.at[k], load_sem.at[0, k])
        far.start()
        near = pltpu.make_async_copy(parts.at[core, :, line_of(k)], near_part.at[k], load_sem.at[1, k])
        near.start()
        loads[k] = (far, near)
    mine = pl.ds(pl.multiple_of(core * height, height), height)
    theirs = pl.ds(pl.multiple_of(other * height, height), height)
    moved = ((stat_in, stat), (basis_in, basis), (first_in, first), (second_in, second), (weights_in, weights))
    keeps = []
    for at, (source, target) in enumerate(moved):
        keep = pltpu.make_async_copy(source.at[core], target.at[mine], keep_sem.at[at])
        keep.start()
        keeps.append(keep)

    barrier = pltpu.get_barrier_semaphore()
    partners = [(rep, other)]
    partners += [(layer * PLANE + spot_of(j), core) for j in range(1, PLANE)]
    partners += [(line_of(k) * PLANE + spot, core) for k in range(1, LINE)]
    for partner in partners:
        pl.semaphore_signal(barrier, inc=1, device_id=partner, device_id_type=MESH)
    pl.semaphore_wait(barrier, len(partners))

    def send(source, target, sems, partner):
        copy = pltpu.make_async_remote_copy(
            src_ref=source, dst_ref=target, send_sem=sems.at[0], recv_sem=sems.at[1],
            device_id=partner, device_id_type=MESH,
        )
        copy.start()
        return copy

    pairs = {}
    for k in ORDER:
        loads[k][0].wait()
        pair_send[k] = far_part[k].astype(BF16)
        pairs[k] = send(pair_send.at[k], pair_recv.at[k], pair_sem.at[k], (rep, other))

    planes = {}
    for k in ORDER:
        loads[k][1].wait()
        pairs[k].wait_recv()
        near_part[k] = near_part[k] + pair_recv[k].astype(F32)
        chip_low[k] = near_part[k].astype(BF16)
        for j in (2, 1, 3):
            planes[k, j] = send(
                chip_low.at[k, spot_of(j)], plane_recv.at[k, j - 1], plane_sem.at[k, j - 1],
                (layer * PLANE + spot_of(j), core),
            )

    swaps = []
    for at, (source, target) in enumerate(moved):
        swaps.append(send(source.at[other], target.at[mine], swap_sem.at[at], (rep, other)))

    lines = {}
    total = None
    for k in ORDER:
        for j in range(1, PLANE):
            planes[k, j].wait_recv()
        total = near_part[k, spot]
        for j in range(1, PLANE):
            total = total + plane_recv[k, j - 1].astype(F32)
        if k:
            line_send[k - 1] = total.astype(BF16)
            lines[k] = send(
                line_send.at[k - 1], line_recv.at[k - 1], line_sem.at[k - 1],
                (line_of(k) * PLANE + spot, core),
            )
    for k in range(1, LINE):
        lines[k].wait_recv()
        total = total + line_recv[k - 1].astype(F32)
    own = rows_of(spot, layer)
    grad[core, own, :] = (total * (1.0 / (PLANE * LINE))).astype(BF16)

    def share(rows, sems, partner):
        return send(grad.at[core, rows], grad.at[core, rows], sems, partner)

    glines = {k: share(own, gline_sem.at[k - 1], (line_of(k) * PLANE + spot, core)) for k in (2, 1, 3)}
    gplanes = {}
    gpairs = []
    for at, k in enumerate((0, 1, 3, 2)):
        rows = rows_of(spot, lax.rem(layer + LINE - k, LINE))
        if k:
            glines[k].wait_recv()
        for j in (2, 1, 3):
            gplanes[k, j] = share(rows, gplane_sem.at[k, j - 1], (layer * PLANE + spot_of(j), core))
        gpairs.append(share(rows, gpair_sem.at[k, 0], (rep, other)))
        if at == 0:
            for step in (0, 1):
                swaps[step].wait_recv()
                keeps[step].wait()
        rows = pl.ds(at * (size // LINE), size // LINE)
        power[rows, :] = stat_beta * dot(stat[rows, :].astype(BF16), basis[...])
    for k in (0, 1, 3, 2):
        for j in (1, 3, 2):
            gplanes[k, j].wait_recv()
            rows = rows_of(lax.rem(spot + PLANE - j, PLANE), lax.rem(layer + LINE - k, LINE))
            gpairs.append(share(rows, gpair_sem.at[k, j], (rep, other)))
    for step in (2, 3, 4):
        swaps[step].wait_recv()
        keeps[step].wait()

    @pl.loop(0, size // tile)
    def _(at):
        rows = tile_rows(at, tile)
        turned = dot(basis[:, rows], grad[core], ((0,), (0,))).astype(BF16)
        rot[rows, :] = turned
        rotated = dot(turned, right[...])
        moment = moment_decay * first[rows, :] + (1.0 - moment_decay) * rotated
        square = square_decay * second[rows, :] + (1.0 - square_decay) * rotated * rotated
        first[rows, :] = moment
        second[rows, :] = square
        direction = moment / (jnp.sqrt(square) + epsilon)
        half[rows, :] = dot(direction.astype(BF16), right[...], ((1,), (1,))).astype(BF16)

    @pl.loop(0, size // tile)
    def _(at):
        rows = tile_rows(at, tile)
        update = dot(basis[rows, :], half[...])
        weights[rows, :] = (weights[rows, :].astype(F32) - learn_rate * update).astype(BF16)

    gives = []
    stores = []

    def store(source, target):
        copy = pltpu.make_async_copy(source, target, store_sem.at[len(stores)])
        copy.start()
        stores.append(copy)

    def give(source, target):
        gives.append(send(source, target, give_sem.at[len(gives)], (rep, other)))

    give(weights, weights_out.at[core])
    give(first.at[theirs], first_out.at[core])
    give(second.at[theirs], second_out.at[core])
    store(weights, weights_out.at[core])
    store(first.at[mine], first_out.at[core])
    store(second.at[mine], second_out.at[core])

    def left_tile(at, squares):
        rows = tile_rows(at, tile)
        value = power[rows, :] + (1.0 - stat_beta) * dot(grad[core, rows, :], rot[...], ((1,), (1,)))
        power[rows, :] = value
        return squares + jnp.sum(value * value)

    squares = lax.fori_loop(0, size // tile, left_tile, jnp.float32(0.0))
    scale = lax.rsqrt(squares + norm_epsilon)

    @pl.loop(0, size // tile)
    def _(at):
        rows = tile_rows(at, tile)
        start[rows, :] = (power[rows, :] * scale).astype(BF16)

    left = schulz_sweeps(start, gram, spare, size, 512)
    give(left.at[theirs], basis_out.at[core])
    store(left.at[mine], basis_out.at[core])

    for copy in gpairs:
        copy.wait_recv()
    width = right.shape[0]

    def right_tile(at, squares):
        rows = tile_rows(at, tile)
        terms = dot(grad[0, :, rows], grad[0], ((0,), (0,))) + dot(grad[1, :, rows], grad[1], ((0,), (0,)))
        mixed = stat_beta * stat_right[rows, :] + (1.0 - stat_beta) * terms
        value = dot(mixed.astype(BF16), right[...])
        rpower[rows, :] = value
        return squares + jnp.sum(value * value)

    rsquares = lax.fori_loop(0, width // tile, right_tile, jnp.float32(0.0))
    rscale = lax.rsqrt(rsquares + norm_epsilon)
    rstart[...] = (rpower[...] * rscale).astype(BF16)
    right_out[...] = schulz_sweeps(rstart, rgram, rspare, width, 512)[...]

    for copy in gives:
        copy.wait_recv()
    for group in (pairs, planes, lines, glines, gplanes):
        for copy in group.values():
            copy.wait_send()
    for copy in gpairs + swaps + gives:
        copy.wait_send()
    for copy in stores:
        copy.wait()


def on_device_blocks(
    grad_parts, weights, stat_left, stat_right, basis_left, basis_right, moment_first, moment_second
):
    blocks, height, width = weights.shape
    size = blocks * height
    piece = size // (PLANE * LINE)
    parts = grad_parts.reshape(blocks, PLANE, LINE, piece, width)
    anywhere = pl.BlockSpec(memory_space=pl.ANY)
    in_vmem = pl.BlockSpec(memory_space=pltpu.VMEM)
    dma = pltpu.SemaphoreType.DMA
    return pl.pallas_call(
        step_kernel,
        out_shape=(
            jax.ShapeDtypeStruct((blocks, size, width), BF16),
            jax.ShapeDtypeStruct((blocks, height, size), BF16),
            jax.ShapeDtypeStruct((width, width), BF16),
            jax.ShapeDtypeStruct((blocks, height, width), F32),
            jax.ShapeDtypeStruct((blocks, height, width), F32),
        ),
        in_specs=[anywhere, anywhere, anywhere, in_vmem, anywhere, in_vmem, anywhere, anywhere],
        out_specs=(anywhere, anywhere, in_vmem, anywhere, anywhere),
        scratch_shapes=[
            pltpu.VMEM((LINE, PLANE, piece, width), F32),
            pltpu.VMEM((LINE, PLANE, piece, width), F32),
            pltpu.VMEM((LINE, PLANE, piece, width), BF16),
            pltpu.VMEM((LINE, PLANE, piece, width), BF16),
            pltpu.VMEM((LINE, PLANE, piece, width), BF16),
            pltpu.VMEM((LINE, PLANE - 1, piece, width), BF16),
            pltpu.VMEM((LINE - 1, piece, width), BF16),
            pltpu.VMEM((LINE - 1, piece, width), BF16),
            pltpu.VMEM((blocks, size, width), BF16),
            pltpu.VMEM((size, size), BF16),
            pltpu.VMEM((size, size), F32),
            pltpu.VMEM((size, width), F32),
            pltpu.VMEM((size, width), F32),
            pltpu.VMEM((size, width), BF16),
            pltpu.VMEM((size, size), F32),
            pltpu.VMEM((size, width), BF16),
            pltpu.VMEM((size, width), BF16),
            pltpu.VMEM((size, size), BF16),
            pltpu.VMEM((size, size), BF16),
            pltpu.VMEM((size, size), BF16),
            pltpu.VMEM((width, width), F32),
            pltpu.VMEM((width, width), BF16),
            pltpu.VMEM((width, width), BF16),
            pltpu.VMEM((width, width), BF16),
            dma((2, LINE)),
            dma((LINE, 2)),
            dma((LINE, PLANE - 1, 2)),
            dma((LINE - 1, 2)),
            dma((LINE - 1, 2)),
            dma((LINE, PLANE - 1, 2)),
            dma((LINE, PLANE, 2)),
            dma((5, 2)),
            dma((5,)),
            dma((4, 2)),
            dma((4,)),
        ],
        compiler_params=pltpu.CompilerParams(
            collective_id=0, has_side_effects=True, vmem_limit_bytes=60 << 20
        ),
    )(parts, weights, stat_left, stat_right, basis_left, basis_right, moment_first, moment_second)


def solution(mesh):
    fits = mesh.shape["shard"] == 2 and mesh.shape["rep"] == 16
    body = on_device_blocks if fits else on_device
    placed = (
        P("rep", "shard", None, None, None),
        P(None, "shard", None),
        P(None, "shard", None),
        P(),
        P(None, "shard", None),
        P(),
        P(None, "shard", None),
        P(None, "shard", None),
    )
    return jax.shard_map(
        body,
        mesh=mesh,
        in_specs=placed,
        out_specs=(
            P(),
            P(None, "shard", None),
            P(),
            P(None, "shard", None),
            P(None, "shard", None),
        ),
        check_vma=False,
    )
```

```python
import functools

import jax
import jax.numpy as jnp
from jax import lax
from jax.experimental import pallas as pl
from jax.experimental.pallas import tpu as pltpu
from jax.sharding import PartitionSpec as P

NS_ITERS = 3


stat_beta = 0.9
moment_decay = 0.9
square_decay = 0.95
learn_rate = 0.1
epsilon = 1e-08
norm_epsilon = 1e-06
schulz_linear = 3.4445
schulz_cubic = -4.775
schulz_quintic = 2.0315


def schulz_whole(matrix):
    current = matrix
    for sweep_index in range(NS_ITERS):
        gram_matrix = lax.optimization_barrier(
            jnp.dot(current, current.T, preferred_element_type=jnp.float32).astype(jnp.bfloat16)
        )
        poly_matrix = (
            schulz_cubic * gram_matrix.astype(jnp.float32)
            + schulz_quintic * jnp.dot(gram_matrix, gram_matrix, preferred_element_type=jnp.float32)
        ).astype(jnp.bfloat16)
        current = (
            schulz_linear * current.astype(jnp.float32)
            + jnp.dot(poly_matrix, current, preferred_element_type=jnp.float32)
        ).astype(jnp.bfloat16)
    return current


def schulz_split(start_rows):
    current = start_rows
    for sweep_index in range(NS_ITERS):
        gathered = lax.all_gather(current, "shard", axis=1, tiled=True)
        gram_rows = lax.optimization_barrier(
            jnp.einsum(
                "bik,bjk->bij", current, gathered, preferred_element_type=jnp.float32
            ).astype(jnp.bfloat16)
        )
        gram_block = lax.all_gather(gram_rows, "shard", axis=1, tiled=True)
        poly_rows = (
            schulz_cubic * gram_rows.astype(jnp.float32)
            + schulz_quintic
            * jnp.einsum("bij,bjk->bik", gram_rows, gram_block, preferred_element_type=jnp.float32)
        ).astype(jnp.bfloat16)
        current = (
            schulz_linear * current.astype(jnp.float32)
            + jnp.einsum("bij,bjk->bik", poly_rows, gathered, preferred_element_type=jnp.float32)
        ).astype(jnp.bfloat16)
    return current


def on_device(
    grad_parts, weights, stat_left, stat_right, basis_left, basis_right, moment_first, moment_second
):
    block_count = weights.shape[0]
    row_count = weights.shape[1]
    width_kv = weights.shape[2]
    rep_count = lax.axis_size("rep")
    shard_pos = lax.axis_index("shard")
    row_start = shard_pos * row_count
    partial_value = grad_parts[0, 0]
    grad_total = lax.psum(partial_value, ("rep", "shard")) / rep_count
    grad_full = grad_total.astype(jnp.bfloat16)
    grad_rows = lax.dynamic_slice_in_dim(grad_full, row_start, row_count, 1)
    left_new = stat_beta * stat_left + (1.0 - stat_beta) * jnp.einsum(
        "bik,bjk->bij", grad_rows, grad_full, preferred_element_type=jnp.float32
    )
    grad_flat = grad_rows.reshape(block_count * row_count, width_kv)
    right_terms = jnp.dot(grad_flat.T, grad_flat, preferred_element_type=jnp.float32)
    right_new = stat_beta * stat_right + (1.0 - stat_beta) * lax.psum(right_terms, "shard")
    basis_all = lax.all_gather(basis_left, "shard", axis=1, tiled=True)
    power_rows = jnp.einsum(
        "bij,bjk->bik", left_new.astype(jnp.bfloat16), basis_all, preferred_element_type=jnp.float32
    )
    local_squares = jnp.sum(power_rows * power_rows, axis=(1, 2))
    block_squares = lax.psum(local_squares, "shard")
    start_rows = (power_rows * lax.rsqrt(block_squares + norm_epsilon)[:, None, None]).astype(
        jnp.bfloat16
    )
    basis_left_new = schulz_split(start_rows)
    right_power = jnp.dot(
        right_new.astype(jnp.bfloat16), basis_right, preferred_element_type=jnp.float32
    )
    right_start = (
        right_power * lax.rsqrt(jnp.sum(right_power * right_power) + norm_epsilon)
    ).astype(jnp.bfloat16)
    basis_right_new = schulz_whole(right_start)
    local_turn = jnp.einsum(
        "bji,bjk->bik", basis_left, grad_rows, preferred_element_type=jnp.float32
    )
    rot_left = lax.psum_scatter(
        local_turn.astype(jnp.bfloat16), "shard", scatter_dimension=1, tiled=True
    ).astype(jnp.float32)
    rot_flat = rot_left.reshape(block_count * row_count, width_kv).astype(jnp.bfloat16)
    rotated = jnp.dot(rot_flat, basis_right, preferred_element_type=jnp.float32).reshape(
        block_count, row_count, width_kv
    )
    moment_new = moment_decay * moment_first + (1.0 - moment_decay) * rotated
    square_new = square_decay * moment_second + (1.0 - square_decay) * rotated * rotated
    direction = moment_new / (jnp.sqrt(square_new) + epsilon)
    direction_flat = direction.reshape(block_count * row_count, width_kv).astype(jnp.bfloat16)
    half_turn = (
        jnp.dot(direction_flat, basis_right.T, preferred_element_type=jnp.float32)
        .astype(jnp.bfloat16)
        .reshape(block_count, row_count, width_kv)
    )
    half_all = lax.all_gather(half_turn, "shard", axis=1, tiled=True)
    update = jnp.einsum("bij,bjk->bik", basis_left, half_all, preferred_element_type=jnp.float32)
    weight_rows_new = (weights.astype(jnp.float32) - learn_rate * update).astype(jnp.bfloat16)
    weights_new = lax.all_gather(weight_rows_new, "shard", axis=1, tiled=True)
    return (weights_new, basis_left_new, basis_right_new, moment_new, square_new)


MESH = pl.DeviceIdType.MESH
PLANE = 4
LINE = 4
ORDER = (2, 1, 3, 0)
F32 = jnp.float32
BF16 = jnp.bfloat16


def dot(a, b, dims=((1,), (0,))):
    return lax.dot_general(a, b, (dims, ((), ())), preferred_element_type=F32)


def tile_rows(at, tile):
    return pl.ds(pl.multiple_of(at * tile, tile), tile)


def schulz_sweeps(start, gram, spare, size, tile):
    chain = (start, spare, start, spare)
    for sweep in range(NS_ITERS):
        now, later = chain[sweep % 2], chain[sweep % 2 + 1]

        @pl.loop(0, size // tile)
        def _(at):
            rows = tile_rows(at, tile)
            gram[rows, :] = dot(now[rows, :], now[...], ((1,), (1,))).astype(BF16)

        @pl.loop(0, size // tile)
        def _(at):
            rows = tile_rows(at, tile)
            poly = schulz_cubic * gram[rows, :].astype(F32) + schulz_quintic * dot(gram[rows, :], gram[...])
            later[rows, :] = (
                schulz_linear * now[rows, :].astype(F32) + dot(poly.astype(BF16), now[...])
            ).astype(BF16)
    return later


def step_kernel(
    parts, weights_in, stat_in, stat_right, basis_in, right, first_in, second_in,
    weights_out, basis_out, right_out, first_out, second_out,
    far_part, near_part, pair_send, pair_recv, chip_low, plane_recv, line_send, line_recv,
    grad, basis, stat, first, second, weights,
    power, rot, rot_sum, half, start, spare, gram, rpower, rterm,
    load_sem, pair_sem, plane_sem, line_sem, gline_sem, gplane_sem, gpair_sem, swap_sem, keep_sem,
    give_sem, store_sem,
):
    rep = lax.axis_index("rep")
    core = lax.axis_index("shard")
    other = 1 - core
    layer = rep // PLANE
    spot = lax.rem(rep, PLANE)
    size = basis.shape[0]
    height = basis_in.shape[1]
    piece = size // (PLANE * LINE)
    tile = 256

    def line_of(k):
        return lax.rem(layer + k, LINE)

    def spot_of(j):
        return lax.rem(spot + j, PLANE)

    def rows_of(p, z):
        return pl.ds(pl.multiple_of((z * PLANE + p) * piece, piece), piece)

    loads = {}
    for k in ORDER:
        far = pltpu.make_async_copy(parts.at[other, line_of(k)], far_part.at[k], load_sem.at[0, k])
        far.start()
        near = pltpu.make_async_copy(parts.at[core, line_of(k)], near_part.at[k], load_sem.at[1, k])
        near.start()
        loads[k] = (far, near)
    mine = pl.ds(pl.multiple_of(core * height, height), height)
    theirs = pl.ds(pl.multiple_of(other * height, height), height)
    moved = ((stat_in, stat), (basis_in, basis), (first_in, first), (second_in, second), (weights_in, weights))
    keeps = []
    for at, (source, target) in enumerate(moved):
        keep = pltpu.make_async_copy(source.at[core], target.at[mine], keep_sem.at[at])
        keep.start()
        keeps.append(keep)

    barrier = pltpu.get_barrier_semaphore()
    partners = [(rep, other)]
    partners += [(layer * PLANE + spot_of(j), core) for j in range(1, PLANE)]
    partners += [(line_of(k) * PLANE + spot, core) for k in range(1, LINE)]
    for partner in partners:
        pl.semaphore_signal(barrier, inc=1, device_id=partner, device_id_type=MESH)
    pl.semaphore_wait(barrier, len(partners))

    def send(source, target, sems, partner):
        copy = pltpu.make_async_remote_copy(
            src_ref=source, dst_ref=target, send_sem=sems.at[0], recv_sem=sems.at[1],
            device_id=partner, device_id_type=MESH,
        )
        copy.start()
        return copy

    pairs = {}
    for k in ORDER:
        loads[k][0].wait()
        pair_send[k] = far_part[k].astype(BF16)
        pairs[k] = send(pair_send.at[k], pair_recv.at[k], pair_sem.at[k], (rep, other))

    planes = {}
    for k in ORDER:
        loads[k][1].wait()
        pairs[k].wait_recv()
        near_part[k] = near_part[k] + pair_recv[k].astype(F32)
        chip_low[k] = near_part[k].astype(BF16)
        for j in (2, 1, 3):
            planes[k, j] = send(
                chip_low.at[k, spot_of(j)], plane_recv.at[k, j - 1], plane_sem.at[k, j - 1],
                (layer * PLANE + spot_of(j), core),
            )

    swaps = []
    for at, (source, target) in enumerate(moved):
        swaps.append(send(source.at[other], target.at[mine], swap_sem.at[at], (rep, other)))

    lines = {}
    total = None
    for k in ORDER:
        for j in range(1, PLANE):
            planes[k, j].wait_recv()
        total = near_part[k, spot]
        for j in range(1, PLANE):
            total = total + plane_recv[k, j - 1].astype(F32)
        if k:
            line_send[k - 1] = total.astype(BF16)
            lines[k] = send(
                line_send.at[k - 1], line_recv.at[k - 1], line_sem.at[k - 1],
                (line_of(k) * PLANE + spot, core),
            )
    for k in range(1, LINE):
        lines[k].wait_recv()
        total = total + line_recv[k - 1].astype(F32)
    own = rows_of(spot, layer)
    grad[core, own, :] = (total * (1.0 / (PLANE * LINE))).astype(BF16)

    def share(rows, sems, partner):
        return send(grad.at[core, rows], grad.at[core, rows], sems, partner)

    glines = {k: share(own, gline_sem.at[k - 1], (line_of(k) * PLANE + spot, core)) for k in (2, 1, 3)}
    gplanes = {}
    gpairs = []
    for at, k in enumerate((0, 1, 3, 2)):
        rows = rows_of(spot, lax.rem(layer + LINE - k, LINE))
        if k:
            glines[k].wait_recv()
        for j in (2, 1, 3):
            gplanes[k, j] = share(rows, gplane_sem.at[k, j - 1], (layer * PLANE + spot_of(j), core))
        gpairs.append(share(rows, gpair_sem.at[k, 0], (rep, other)))
        if at == 0:
            for step in (0, 1):
                swaps[step].wait_recv()
                keeps[step].wait()
        rows = pl.ds(at * (size // LINE), size // LINE)
        power[rows, :] = stat_beta * dot(stat[rows, :].astype(BF16), basis[...])
    for k in (0, 1, 3, 2):
        for j in (1, 3, 2):
            gplanes[k, j].wait_recv()
            rows = rows_of(lax.rem(spot + PLANE - j, PLANE), lax.rem(layer + LINE - k, LINE))
            gpairs.append(share(rows, gpair_sem.at[k, j], (rep, other)))
        group = tile_rows(lax.rem(layer + LINE - k, LINE), size // LINE)
        if k == 0:
            rterm[...] = dot(grad[core, group, :], grad[core, group, :], ((0,), (0,)))
        else:
            rterm[...] += dot(grad[core, group, :], grad[core, group, :], ((0,), (0,)))

        @pl.loop(0, size // tile)
        def _(at):
            rows = tile_rows(at, tile)
            added = dot(basis[group, rows], grad[core, group, :], ((0,), (0,)))
            if k == 0:
                rot_sum[rows, :] = added
            else:
                rot_sum[rows, :] += added
    for step in (2, 3, 4):
        swaps[step].wait_recv()
        keeps[step].wait()

    @pl.loop(0, size // tile)
    def _(at):
        rows = tile_rows(at, tile)
        turned = rot_sum[rows, :].astype(BF16)
        rot[rows, :] = turned
        rotated = dot(turned, right[...])
        moment = moment_decay * first[rows, :] + (1.0 - moment_decay) * rotated
        square = square_decay * second[rows, :] + (1.0 - square_decay) * rotated * rotated
        first[rows, :] = moment
        second[rows, :] = square
        direction = moment / (jnp.sqrt(square) + epsilon)
        half[rows, :] = dot(direction.astype(BF16), right[...], ((1,), (1,))).astype(BF16)

    @pl.loop(0, size // tile)
    def _(at):
        rows = tile_rows(at, tile)
        update = dot(basis[rows, :], half[...])
        weights[rows, :] = (weights[rows, :].astype(F32) - learn_rate * update).astype(BF16)

    gives = []
    stores = []

    def store(source, target):
        copy = pltpu.make_async_copy(source, target, store_sem.at[len(stores)])
        copy.start()
        stores.append(copy)

    def give(source, target):
        gives.append(send(source, target, give_sem.at[len(gives)], (rep, other)))

    give(weights, weights_out.at[core])
    give(first.at[theirs], first_out.at[core])
    give(second.at[theirs], second_out.at[core])
    store(weights, weights_out.at[core])
    store(first.at[mine], first_out.at[core])
    store(second.at[mine], second_out.at[core])

    def left_tile(at, squares):
        rows = tile_rows(at, tile)
        value = power[rows, :] + (1.0 - stat_beta) * dot(grad[core, rows, :], rot[...], ((1,), (1,)))
        power[rows, :] = value
        return squares + jnp.sum(value * value)

    squares = lax.fori_loop(0, size // tile, left_tile, jnp.float32(0.0))
    scale = lax.rsqrt(squares + norm_epsilon)

    @pl.loop(0, size // tile)
    def _(at):
        rows = tile_rows(at, tile)
        start[rows, :] = (power[rows, :] * scale).astype(BF16)

    left = schulz_sweeps(start, gram, spare, size, size)
    give(left.at[theirs], basis_out.at[core])
    store(left.at[mine], basis_out.at[core])

    for copy in gpairs:
        copy.wait_recv()
    width = right.shape[0]

    def right_tile(at, squares):
        rows = tile_rows(at, tile)
        terms = rterm[rows, :] + dot(grad[other, :, rows], grad[other], ((0,), (0,)))
        mixed = stat_beta * stat_right[rows, :] + (1.0 - stat_beta) * terms
        value = dot(mixed.astype(BF16), right[...])
        rpower[rows, :] = value
        return squares + jnp.sum(value * value)

    rsquares = lax.fori_loop(0, width // tile, right_tile, jnp.float32(0.0))
    rscale = lax.rsqrt(rsquares + norm_epsilon)
    right_out[...] = (rpower[...] * rscale).astype(BF16)

    for copy in gives:
        copy.wait_recv()
    for group in (pairs, planes, lines, glines, gplanes):
        for copy in group.values():
            copy.wait_send()
    for copy in gpairs + swaps + gives:
        copy.wait_send()
    for copy in stores:
        copy.wait()


def finish_kernel(
    start, weights, basis, first, second, right_out, weights_out, basis_out, first_out, second_out,
    hold_weights, hold_basis, hold_first, hold_second, now, spare, gram, load_sem, store_sem,
):
    moves = (
        (weights, hold_weights, weights_out),
        (basis, hold_basis, basis_out),
        (first, hold_first, first_out),
        (second, hold_second, second_out),
    )
    loads = []
    stores = []
    for at, (source, hold, target) in enumerate(moves):
        load = pltpu.make_async_copy(source, hold, load_sem.at[at])
        load.start()
        loads.append(load)
    now[...] = start[...]
    for at, (source, hold, target) in enumerate(moves):
        loads[at].wait()
        store = pltpu.make_async_copy(hold, target, store_sem.at[at])
        store.start()
        stores.append(store)
    right_out[...] = schulz_sweeps(now, gram, spare, now.shape[0], now.shape[0])[...]
    for store in stores:
        store.wait()


def finish_right(start, *held):
    anywhere = pl.BlockSpec(memory_space=pl.ANY)
    in_vmem = pl.BlockSpec(memory_space=pltpu.VMEM)
    dma = pltpu.SemaphoreType.DMA
    width = start.shape[0]
    return pl.pallas_call(
        finish_kernel,
        out_shape=[jax.ShapeDtypeStruct(a.shape, a.dtype) for a in (start,) + held],
        in_specs=[in_vmem] + [anywhere] * 4,
        out_specs=[in_vmem] + [anywhere] * 4,
        scratch_shapes=[pltpu.VMEM(a.shape, a.dtype) for a in held]
        + [pltpu.VMEM((width, width), BF16)] * 3
        + [dma((4,)), dma((4,))],
        compiler_params=pltpu.CompilerParams(vmem_limit_bytes=62 << 20),
    )(start, *held)


def on_device_blocks(
    grad_parts, weights, stat_left, stat_right, basis_left, basis_right, moment_first, moment_second
):
    blocks, height, width = weights.shape
    size = blocks * height
    piece = size // (PLANE * LINE)
    parts = grad_parts.reshape(blocks, LINE, PLANE, piece, width)
    anywhere = pl.BlockSpec(memory_space=pl.ANY)
    in_vmem = pl.BlockSpec(memory_space=pltpu.VMEM)
    dma = pltpu.SemaphoreType.DMA
    weights_new, left_new, right_start, first_new, second_new = pl.pallas_call(
        step_kernel,
        out_shape=(
            jax.ShapeDtypeStruct((blocks, size, width), BF16),
            jax.ShapeDtypeStruct((blocks, height, size), BF16),
            jax.ShapeDtypeStruct((width, width), BF16),
            jax.ShapeDtypeStruct((blocks, height, width), F32),
            jax.ShapeDtypeStruct((blocks, height, width), F32),
        ),
        in_specs=[anywhere, anywhere, anywhere, in_vmem, anywhere, in_vmem, anywhere, anywhere],
        out_specs=(anywhere, anywhere, in_vmem, anywhere, anywhere),
        scratch_shapes=[
            pltpu.VMEM((LINE, PLANE, piece, width), F32),
            pltpu.VMEM((LINE, PLANE, piece, width), F32),
            pltpu.VMEM((LINE, PLANE, piece, width), BF16),
            pltpu.VMEM((LINE, PLANE, piece, width), BF16),
            pltpu.VMEM((LINE, PLANE, piece, width), BF16),
            pltpu.VMEM((LINE, PLANE - 1, piece, width), BF16),
            pltpu.VMEM((LINE - 1, piece, width), BF16),
            pltpu.VMEM((LINE - 1, piece, width), BF16),
            pltpu.VMEM((blocks, size, width), BF16),
            pltpu.VMEM((size, size), BF16),
            pltpu.VMEM((size, size), F32),
            pltpu.VMEM((size, width), F32),
            pltpu.VMEM((size, width), F32),
            pltpu.VMEM((size, width), BF16),
            pltpu.VMEM((size, size), F32),
            pltpu.VMEM((size, width), BF16),
            pltpu.VMEM((size, width), F32),
            pltpu.VMEM((size, width), BF16),
            pltpu.VMEM((size, size), BF16),
            pltpu.VMEM((size, size), BF16),
            pltpu.VMEM((size, size), BF16),
            pltpu.VMEM((width, width), F32),
            pltpu.VMEM((width, width), F32),
            dma((2, LINE)),
            dma((LINE, 2)),
            dma((LINE, PLANE - 1, 2)),
            dma((LINE - 1, 2)),
            dma((LINE - 1, 2)),
            dma((LINE, PLANE - 1, 2)),
            dma((LINE, PLANE, 2)),
            dma((5, 2)),
            dma((5,)),
            dma((4, 2)),
            dma((4,)),
        ],
        compiler_params=pltpu.CompilerParams(
            collective_id=0, has_side_effects=True, vmem_limit_bytes=60 << 20
        ),
    )(parts, weights, stat_left, stat_right, basis_left, basis_right, moment_first, moment_second)
    right_new, weights_new, left_new, first_new, second_new = finish_right(
        right_start, weights_new, left_new, first_new, second_new
    )
    return weights_new, left_new, right_new, first_new, second_new


def solution(mesh):
    fits = mesh.shape["shard"] == 2 and mesh.shape["rep"] == 16
    body = on_device_blocks if fits else on_device
    placed = (
        P("rep", "shard", None, None, None),
        P(None, "shard", None),
        P(None, "shard", None),
        P(),
        P(None, "shard", None),
        P(),
        P(None, "shard", None),
        P(None, "shard", None),
    )
    return jax.shard_map(
        body,
        mesh=mesh,
        in_specs=placed,
        out_specs=(
            P(),
            P(None, "shard", None),
            P(),
            P(None, "shard", None),
            P(None, "shard", None),
        ),
        check_vma=False,
    )
```
